256 devices in a mesh: reg: 128 (over z, x, y), bat: 2 (over core).
Axes of the slice: x: 4, y: 4, z: 8, core: 2. Of those that a mesh axis runs over, the one named last changes fastest.
Arguments:
- top_flow: float32 [256, 32768], P('reg', 'bat'), may hold values from 0.25 to 4
- mid_logprob: float32 [384, 32768], P('reg', 'bat'), may hold values from -420 to -30
- low_logprob: float32 [512, 32768], P('reg', 'bat'), may hold values from -420 to -30
- top_weight: bfloat16 [256, 64, 4096], P('reg'), may hold values from 0.049804688 to 1
- mid_weight: bfloat16 [384, 64, 4096], P('reg'), may hold values from 0.049804688 to 1
- top_children: int32 [256, 2], replicated, may hold values from 0 to 383, all different within a row
- mid_children: int32 [384, 2], replicated, may hold values from 0 to 511, all different within a row
Outputs:
- low_flow: float32 [512, 32768], P('reg', 'bat')
- top_params: float32 [256, 64, 4096], P('reg', 'bat')
- mid_params: float32 [384, 64, 4096], P('reg', 'bat')
The draws below stay inside these ranges and needn't reach their ends.
Inputs may be any that keep to these rules, and one draw needn't show every extreme that they name: `top_children`: each row names two different middle regions, and every middle region is named by some row. `mid_children`: each row names two different lower regions, and every lower region is named by some row.
All inputs are finite; a program needn't handle non-finite values.
Results may differ from the reference program's by a relative error of at most 0.0024.
Values may be sent and summed in bfloat16 or wider, within the bound.
A program may use at most 64 MiB of HBM per device.

```python
import math
import jax
import jax.numpy as jnp
from jax import lax

K = 64
NTOP = 256
NMID = 384
NLOW = 512
BATCH = 512


def log_values(key, region_count):
    key_offset, key_jitter = jax.random.split(key)
    offset = jax.random.uniform(key_offset, (region_count, BATCH, 1), jnp.float32, -350.0, -40.0)
    jitter = jnp.clip(1.5 * jax.random.normal(key_jitter, (region_count, BATCH, K), jnp.float32), -9.0, 9.0)
    return (offset + jitter).reshape(region_count, BATCH * K)


def draw_mid_logprob(key, part):
    return log_values(jax.random.fold_in(key, 17), NMID)


def draw_low_logprob(key, part):
    return log_values(jax.random.fold_in(key, 29), NLOW)


def steps_of(key, dims, cuts, smallest, high):
    def one(position, blocks):
        heights = jax.random.uniform(jax.random.fold_in(jax.random.fold_in(key, 6), position), (blocks,), jnp.float32, smallest / len(cuts), high / len(cuts))
        return jnp.repeat(jnp.exp(heights), dims[position] // blocks).reshape((-1,) + (1,) * (len(dims) - position - 1))

    level = one(*cuts[0])
    for cut in cuts[1:]:
        level = level * one(*cut)
    return level


def picks_of(own_key, rows, amount, top, lift):
    sequence = jax.random.permutation(jax.random.fold_in(own_key, 1), amount)
    boost = sequence
    for power in range(3):
        boost = boost * boost // amount
    boost = boost * lift // amount
    chance = jax.random.randint(jax.random.fold_in(own_key, 2), (rows, amount), 0, 4096) + boost
    sure = jax.random.permutation(jax.random.fold_in(own_key, 3), rows)[jnp.arange(amount) % rows]
    chance = jnp.where(jnp.arange(rows)[:, None] == sure[None, :], 1 << 14, chance)
    score = chance * amount + jnp.arange(amount)
    return lax.top_k(score.astype(jnp.int32), top)[1].astype(jnp.int32)


def setup_inputs(seed: int = 0) -> dict:
    key_list = jax.random.split(jax.random.key(seed), 8)
    top_flow = jnp.clip(jnp.exp(math.log(4.0) - 2.7725887 * jax.random.uniform(key_list[0], (NTOP, BATCH * K), jnp.float32) ** steps_of(key_list[0], (NTOP, BATCH * K), ((0, 128), (1, 2)), -0.2, 0.2)), 0.25, 4.0)
    mid_logprob = draw_mid_logprob(jax.random.fold_in(key_list[7], 71), 0)
    low_logprob = draw_low_logprob(jax.random.fold_in(key_list[7], 71), 0)
    top_weight = jnp.clip(jnp.exp(math.log(1.0) - 2.9996462 * jax.random.uniform(key_list[3], (NTOP, K, K * K), jnp.float32) ** steps_of(key_list[3], (NTOP, K, K * K), ((0, 128),), -0.2, 0.2)), 0.049804688, 1.0).astype(jnp.bfloat16)
    mid_weight = jnp.clip(jnp.exp(math.log(1.0) - 2.9996462 * jax.random.uniform(key_list[4], (NMID, K, K * K), jnp.float32) ** steps_of(key_list[4], (NMID, K, K * K), ((0, 128),), -0.2, 0.2)), 0.049804688, 1.0).astype(jnp.bfloat16)
    top_children = picks_of(key_list[5], NTOP, NMID, 2, 85)
    mid_children = picks_of(key_list[6], NMID, NLOW, 2, 64)
    return {"top_flow": top_flow, "mid_logprob": mid_logprob, "low_logprob": low_logprob, "top_weight": top_weight, "mid_weight": mid_weight, "top_children": top_children, "mid_children": mid_children}


def normalized(logprob, region_count):
    tables = logprob.reshape(region_count, BATCH, K)
    return jnp.exp(tables - jnp.max(tables, axis=2, keepdims=True)).astype(jnp.bfloat16)


def region_pass(weight, flows, left_vals, right_vals):
    row_count = left_vals.shape[0]
    left_full = left_vals.astype(jnp.float32)
    right_full = right_vals.astype(jnp.float32)
    outers = (left_full[:, :, None] * right_full[:, None, :]).reshape(row_count, K * K).astype(jnp.bfloat16)
    masses = lax.dot_general(outers, weight, (((1,), (1,)), ((), ())), preferred_element_type=jnp.float32)
    ratios = (flows / masses).astype(jnp.bfloat16)
    spread = jnp.dot(ratios, weight, preferred_element_type=jnp.float32).reshape(row_count, K, K)
    left_flow = left_full * jnp.einsum("xij,xj->xi", spread, right_full)
    right_flow = right_full * jnp.einsum("xij,xi->xj", spread, left_full)
    moment = lax.dot_general(ratios, outers, (((0,), (0,)), ((), ())), preferred_element_type=jnp.float32)
    return left_flow, right_flow, moment * weight.astype(jnp.float32)


def layer(weights, flows, values, children):
    left_vals = jnp.take(values, children[:, 0], axis=0)
    right_vals = jnp.take(values, children[:, 1], axis=0)
    left_flow, right_flow, params = lax.map(
        lambda region_item: region_pass(region_item[0], region_item[1], region_item[2], region_item[3]),
        (weights, flows, left_vals, right_vals))
    ids = jnp.concatenate([children[:, 0], children[:, 1]]).astype(jnp.int32)
    totals = jax.ops.segment_sum(jnp.concatenate([left_flow, right_flow], axis=0), ids, num_segments=values.shape[0])
    return totals, params


def reference(top_flow, mid_logprob, low_logprob, top_weight, mid_weight, top_children, mid_children):
    mid_values = normalized(mid_logprob, NMID)
    low_values = normalized(low_logprob, NLOW)
    mid_flow, top_params = layer(top_weight, top_flow.reshape(NTOP, BATCH, K), mid_values, top_children)
    low_flow, mid_params = layer(mid_weight, mid_flow, low_values, mid_children)
    return low_flow.reshape(NLOW, BATCH * K), top_params, mid_params
```

```python
import functools

import jax
import jax.numpy as jnp
from jax import lax
from jax.experimental import pallas as pl
from jax.experimental.pallas import tpu as pltpu
from jax.sharding import PartitionSpec as P

F32 = jnp.float32
BF16 = jnp.bfloat16
MESH = pl.DeviceIdType.MESH
LANES = 128


def exchange(peers, me, send_buf, recv_buf, send_sem, recv_sem):
    def one(step, carry):
        target = lax.rem(me + step, peers)
        pltpu.make_async_remote_copy(
            src_ref=send_buf.at[target],
            dst_ref=recv_buf.at[me],
            send_sem=send_sem,
            recv_sem=recv_sem,
            device_id={"reg": target},
            device_id_type=MESH,
        ).start()
        return carry

    lax.fori_loop(1, peers, one, 0)
    recv_buf[me] = send_buf[me]


def whole(peers, me, send_buf, recv_buf, send_sem, recv_sem):
    return pltpu.make_async_remote_copy(
        src_ref=send_buf.at[pl.ds(0, peers - 1)],
        dst_ref=recv_buf.at[pl.ds(0, peers - 1)],
        send_sem=send_sem,
        recv_sem=recv_sem,
        device_id={"reg": lax.rem(me + 1, peers)},
        device_id_type=MESH,
    )


def kernel(
    peers,
    comps,
    top_flow, mid_lp, low_lp, top_w, mid_w, top_ch, mid_ch,
    low_out, top_params, mid_params,
    flow_in, mid_in, low_in, tw, mw, tch, mch,
    stage, rows, edge_ids,
    pick_top, sum_top, pick_mid, sum_mid,
    w_turned, outers, lefts, rights, partials, mass_mid, flow_turned, ratios,
    moments, moments_in, params,
    s1m, r1m, s1l, r1l, s2t, r2t, s2m, r2m, s3, r3, s4, r4, s5, r5, s6, r6,
    in_sem, send_sem, recv_sem, mom_send, mom_recv, out_sem,
):
    me = lax.axis_index("reg")
    bat = lax.axis_index("bat")
    other = 1 - bat
    n_top = tw.shape[0]
    n_mid = mw.shape[0]
    n_low = low_in.shape[0]
    half = comps // 2
    pairs = flow_in.shape[1] // LANES
    wide = 2 * LANES

    loads = [
        pltpu.make_async_copy(src, dst, in_sem.at[slot])
        for slot, (src, dst) in enumerate(
            [(mid_lp, mid_in), (low_lp, low_in), (top_ch, tch), (mid_ch, mch),
             (top_flow, flow_in), (top_w, tw), (mid_w, mw)]
        )
    ]
    for load in loads:
        load.start()

    barrier = pltpu.get_barrier_semaphore()

    def greet(step, carry):
        pl.semaphore_signal(
            barrier, inc=1, device_id={"reg": lax.rem(me + step, peers)}, device_id_type=MESH
        )
        return carry

    lax.fori_loop(1, peers, greet, 0)
    pl.semaphore_signal(barrier, inc=1, device_id={"bat": other}, device_id_type=MESH)

    def chunk_rows(source, count):
        def some(group, carry):
            for u in range(8):
                c = group * 8 + u
                stage[pl.ds(pl.multiple_of(c * 8, 8), count), :] = source[
                    :, pl.ds(pl.multiple_of(c * LANES, LANES), LANES)
                ]
            return carry

        lax.fori_loop(0, pairs // 8, some, 0)

    def values_to_send(source, count, send_buf):
        chunk_rows(source, count)
        slots = send_buf.shape[1]
        for q in range(slots):
            if q >= count:
                rows[pl.ds(q, LANES, stride=slots), :] = jnp.zeros((LANES, LANES), F32)
                continue
            turned = stage[pl.ds(q, LANES, stride=8), :].T
            parts = []
            for par in range(2):
                part = turned[par * comps:(par + 1) * comps]
                parts.append(jnp.exp(part - jnp.max(part, axis=0, keepdims=True)))
            rows[pl.ds(q, LANES, stride=slots), :] = jnp.concatenate(parts, axis=0)
        send_buf[...] = rows[0:LANES * slots].astype(send_buf.dtype).reshape(send_buf.shape)

    def edge_table(children, grouped, slots):
        ids = children[...]
        if grouped != slots:
            ids = (ids // grouped) * slots + ids % grouped
        ids = ids.astype(F32)
        for t in range(children.shape[1] // LANES):
            for side in range(2):
                block = jnp.broadcast_to(
                    ids[side:side + 1, t * LANES:(t + 1) * LANES], (LANES, LANES)
                )
                edge_ids[pl.ds(2 * t * LANES + side, LANES, stride=2), :] = block.T

    def pick_table(edges, pick):
        ids = edge_ids[0:edges]
        lane = lax.broadcasted_iota(jnp.int32, (edges, LANES), 1).astype(F32)
        for t in range(pick.shape[1] // LANES):
            pick[:, t * LANES:(t + 1) * LANES] = jnp.where(
                ids == lane + float(t * LANES), 1.0, 0.0
            ).astype(BF16)

    def sum_table(edges, table):
        count = table.shape[0]
        row = lax.broadcasted_iota(jnp.int32, (count, LANES), 0).astype(F32)
        for t in range(edges // LANES):
            turned = edge_ids[t * LANES:(t + 1) * LANES].T
            table[:, t * LANES:(t + 1) * LANES] = jnp.where(
                row == turned[0:1], 1.0, 0.0
            ).astype(BF16)

    def matrix(recv_buf):
        return recv_buf[...].reshape(recv_buf.shape[0] * recv_buf.shape[1], LANES)

    def product(a, b):
        return lax.dot_general(a, b, (((1,), (0,)), ((), ())), preferred_element_type=F32)

    def unpack(recv_buf):
        slots = recv_buf.shape[1]
        rows[0:LANES * slots] = recv_buf[...].astype(F32).reshape(LANES * slots, LANES)

    def wide_row(q, slots):
        return jnp.concatenate(
            [rows[pl.ds(par * comps * slots + q, comps, stride=slots), :] for par in range(2)], axis=1
        )

    def put_wide(q, slots, value):
        for par in range(2):
            rows[pl.ds(par * comps * slots + q, comps, stride=slots), :] = value[
                :, par * LANES:(par + 1) * LANES
            ]

    def pack(send_buf):
        slots = send_buf.shape[1]
        send_buf[...] = rows[0:LANES * slots].astype(send_buf.dtype).reshape(send_buf.shape)

    def build_outer(slot):
        right = rights[slot].astype(BF16).reshape(comps // 16, 16, wide)

        def some(group, carry):
            for u in range(4):
                i = group * 4 + u
                left = jnp.broadcast_to(lefts[slot, pl.ds(i, 1), :], (16, wide)).astype(BF16)
                outers[slot, pl.ds(pl.multiple_of(i * comps, comps), comps), :] = (
                    right * left[None]
                ).reshape(comps, wide)
            return carry

        lax.fori_loop(0, comps // 4, some, 0)

    def flows_of(slot, ratio, q, slots):
        right = rights[slot]

        def block(b, right_acc):
            start = pl.multiple_of(b * 8 * comps, 8 * comps)
            spread = product(w_turned[slot, pl.ds(start, 8 * comps), :], ratio)
            for u in range(8):
                piece = spread[u * comps:(u + 1) * comps]
                left = lefts[slot, pl.ds(b * 8 + u, 1), :]
                right_acc = right_acc + piece * left
                folded = jnp.sum((piece * right).reshape(comps // 8, 8, wide), axis=0)
                at = pl.ds(pl.multiple_of((b * 8 + u) * 8, 8), 8)
                for par in range(2):
                    partials[par, at, :] = folded[:, par * LANES:(par + 1) * LANES]
            return right_acc

        right_acc = lax.fori_loop(0, comps // 8, block, jnp.zeros((comps, wide), F32))
        left_acc = jnp.concatenate(
            [
                functools.reduce(
                    lambda a, b: a + b,
                    [partials[par, pl.ds(sub, comps, stride=8), :] for sub in range(8)],
                )
                for par in range(2)
            ],
            axis=1,
        )
        put_wide(q, slots, left_acc * lefts[slot])
        put_wide(q + 1, slots, right_acc * right)

    def moment_of(slot):
        moments[slot] = lax.dot_general(
            ratios[slot], outers[slot], (((1,), (1,)), ((), ())), preferred_element_type=F32
        )

    def moment_copy(slot):
        return pltpu.make_async_remote_copy(
            src_ref=moments.at[slot, pl.ds(pl.multiple_of(other * half, half), half), :],
            dst_ref=moments_in.at[slot],
            send_sem=mom_send.at[slot],
            recv_sem=mom_recv.at[slot],
            device_id={"bat": other},
            device_id_type=MESH,
        )

    def finish_params(slot, weight):
        moment_copy(slot).wait_recv()
        own = pl.ds(pl.multiple_of(bat * half, half), half)
        params[slot] = (moments[slot, own, :] + moments_in[slot]) * weight[own, :].astype(F32)

    def phase(index, send_buf, recv_buf):
        return (peers, me, send_buf, recv_buf, send_sem.at[index], recv_sem.at[index])

    phases = [
        phase(index, a, b)
        for index, (a, b) in enumerate(
            [(s1m, r1m), (s1l, r1l), (s2t, r2t), (s2m, r2m), (s3, r3), (s4, r4), (s5, r5), (s6, r6)]
        )
    ]

    loads[0].wait()
    values_to_send(mid_in, n_mid, s1m)
    loads[1].wait()
    values_to_send(low_in, n_low, s1l)
    pl.semaphore_wait(barrier, peers)
    exchange(*phases[0])
    exchange(*phases[1])

    loads[2].wait()
    edge_table(tch, n_mid, s1m.shape[1])
    pick_table(pick_top.shape[0], pick_top)

    whole(*phases[0]).wait_recv()
    s2t[...] = product(pick_top[...], matrix(r1m)).astype(BF16).reshape(s2t.shape)
    exchange(*phases[2])

    sum_table(pick_top.shape[0], sum_top)
    loads[3].wait()
    edge_table(mch, n_low, s1l.shape[1])
    pick_table(pick_mid.shape[0], pick_mid)
    whole(*phases[1]).wait_recv()
    s2m[...] = product(pick_mid[...], matrix(r1l)).astype(BF16).reshape(s2m.shape)
    exchange(*phases[3])

    loads[5].wait()
    for r in range(n_top):
        w_turned[r] = tw[r].T
    loads[4].wait()
    chunk_rows(flow_in, n_top)
    for r in range(n_top):
        turned = stage[pl.ds(r, LANES, stride=8), :].T
        flow_turned[r] = jnp.concatenate([turned[0:comps], turned[comps:2 * comps]], axis=1)

    whole(*phases[2]).wait_recv()
    unpack(r2t)
    for r in range(n_top):
        lefts[r] = wide_row(2 * r, 2 * n_top)
        rights[r] = wide_row(2 * r + 1, 2 * n_top)
    for r in range(n_top):
        build_outer(r)
        mass = product(tw[r], outers[r])
        ratio = (flow_turned[r] / mass).astype(BF16)
        ratios[r] = ratio
        flows_of(r, ratio, 2 * r, 2 * n_top)
    pack(s3)
    exchange(*phases[4])

    for r in range(n_top):
        moment_of(r)
        moment_copy(r).start()
    sum_table(pick_mid.shape[0], sum_mid)

    whole(*phases[4]).wait_recv()
    s4[...] = product(sum_top[...], matrix(r3)).reshape(s4.shape)
    exchange(*phases[5])

    loads[6].wait()
    whole(*phases[3]).wait_recv()
    unpack(r2m)
    for r in range(n_mid):
        lefts[n_top + r] = wide_row(2 * r, 2 * n_mid)
        rights[n_top + r] = wide_row(2 * r + 1, 2 * n_mid)
    for r in range(n_mid):
        w_turned[n_top + r] = mw[r].T
        build_outer(n_top + r)
        mass_mid[r] = product(mw[r], outers[n_top + r])

    whole(*phases[5]).wait_recv()
    unpack(r4)
    for r in range(n_mid):
        flow_turned[r] = wide_row(r, r4.shape[1])
    for r in range(n_mid):
        ratio = (flow_turned[r] / mass_mid[r]).astype(BF16)
        ratios[n_top + r] = ratio
        flows_of(n_top + r, ratio, 2 * r, 2 * n_mid)
    pack(s5)
    exchange(*phases[6])

    outs = []
    for r in range(n_top):
        finish_params(r, tw.at[r])
        outs.append(pltpu.make_async_copy(params.at[r], top_params.at[r], out_sem.at[r]))
        outs[-1].start()
    for r in range(n_mid):
        moment_of(n_top + r)
        moment_copy(n_top + r).start()

    whole(*phases[6]).wait_recv()
    s6[...] = product(sum_mid[...], matrix(r5)).reshape(s6.shape)
    exchange(*phases[7])

    for r in range(n_mid):
        slot = n_top + r
        finish_params(slot, mw.at[r])
        outs.append(pltpu.make_async_copy(params.at[slot], mid_params.at[r], out_sem.at[slot]))
        outs[-1].start()

    whole(*phases[7]).wait_recv()
    unpack(r6)
    for q in range(n_low):
        low_out[q] = rows[pl.ds(q, LANES, stride=n_low), :].T

    for one in phases:
        whole(*one).wait_send()
    for slot in range(n_top + n_mid):
        moment_copy(slot).wait_send()
    for out in outs:
        out.wait()


def shards(top_flow, mid_logprob, low_logprob, top_weight, mid_weight, top_children, mid_children):
    peers = lax.axis_size("reg")
    n_top, comps, square = top_weight.shape
    n_mid = mid_weight.shape[0]
    n_low = low_logprob.shape[0]
    n_all = n_top + n_mid
    half = comps // 2
    wide = 2 * LANES
    mid_slots = 4
    top_edges = 2 * n_top
    mid_edges = 2 * n_mid
    vmem = pltpu.VMEM

    def pair(slots, kind=BF16):
        return [vmem((peers, slots, LANES), kind)] * 2

    low, top_params, mid_params = pl.pallas_call(
        functools.partial(kernel, peers, comps),
        out_shape=(
            jax.ShapeDtypeStruct((n_low, LANES, LANES), F32),
            jax.ShapeDtypeStruct((n_top, half, square), F32),
            jax.ShapeDtypeStruct((n_mid, half, square), F32),
        ),
        in_specs=[pl.BlockSpec(memory_space=pltpu.HBM)] * 7,
        out_specs=(
            pl.BlockSpec(memory_space=pltpu.VMEM),
            pl.BlockSpec(memory_space=pl.ANY),
            pl.BlockSpec(memory_space=pl.ANY),
        ),
        scratch_shapes=[
            vmem(top_flow.shape, F32),
            vmem(mid_logprob.shape, F32),
            vmem(low_logprob.shape, F32),
            vmem(top_weight.shape, BF16),
            vmem(mid_weight.shape, BF16),
            vmem(top_children.shape[::-1], jnp.int32),
            vmem(mid_children.shape[::-1], jnp.int32),
            vmem((8 * LANES, LANES), F32),
            vmem((LANES * mid_edges, LANES), F32),
            vmem((peers * mid_edges, LANES), F32),
            vmem((peers * top_edges, peers * mid_slots), BF16),
            vmem((peers * mid_slots, peers * top_edges), BF16),
            vmem((peers * mid_edges, peers * n_low), BF16),
            vmem((peers * n_low, peers * mid_edges), BF16),
            vmem((n_all, square, comps), BF16),
            vmem((n_all, square, wide), BF16),
            vmem((n_all, comps, wide), F32),
            vmem((n_all, comps, wide), F32),
            vmem((2, 8 * comps, LANES), F32),
            vmem((n_mid, comps, wide), F32),
            vmem((n_mid, comps, wide), F32),
            vmem((n_all, comps, wide), BF16),
            vmem((n_all, comps, square), F32),
            vmem((n_all, half, square), F32),
            vmem((n_all, half, square), F32),
            *pair(mid_slots), *pair(n_low), *pair(top_edges), *pair(mid_edges),
            *pair(top_edges), *pair(mid_slots, F32), *pair(mid_edges), *pair(n_low, F32),
            pltpu.SemaphoreType.DMA((7,)),
            pltpu.SemaphoreType.DMA((8,)),
            pltpu.SemaphoreType.DMA((8,)),
            pltpu.SemaphoreType.DMA((n_all,)),
            pltpu.SemaphoreType.DMA((n_all,)),
            pltpu.SemaphoreType.DMA((n_all,)),
        ],
        compiler_params=pltpu.CompilerParams(
            collective_id=0, has_side_effects=True, vmem_limit_bytes=60 * 1024 * 1024
        ),
    )(top_flow, mid_logprob, low_logprob, top_weight, mid_weight, top_children.T, mid_children.T)
    return low.reshape(low_logprob.shape), top_params, mid_params


def solution(mesh):
    return jax.shard_map(
        shards,
        mesh=mesh,
        in_specs=(
            P("reg", "bat"),
            P("reg", "bat"),
            P("reg", "bat"),
            P("reg", None, None),
            P("reg", None, None),
            P(),
            P(),
        ),
        out_specs=(P("reg", "bat"), P("reg", "bat", None), P("reg", "bat", None)),
        check_vma=False,
    )
```

```python
import functools

import jax
import jax.numpy as jnp
from jax import lax
from jax.experimental import pallas as pl
from jax.experimental.pallas import tpu as pltpu
from jax.sharding import PartitionSpec as P

F32 = jnp.float32
BF16 = jnp.bfloat16
MESH = pl.DeviceIdType.MESH
LANES = 128


def each_peer(peers, me, visit):
    def one(step):
        ahead = me + step
        visit(jnp.where(ahead >= peers, ahead - peers, ahead))

    def some(group, carry):
        for u in range(1, 9):
            one(group * 8 + u)
        return carry

    groups = (peers - 1) // 8
    lax.fori_loop(0, groups, some, 0)
    for step in range(groups * 8 + 1, peers):
        one(step)


def exchange(peers, me, send_buf, recv_buf, send_sem, recv_sem):
    def one(target):
        pltpu.make_async_remote_copy(
            src_ref=send_buf.at[target],
            dst_ref=recv_buf.at[me],
            send_sem=send_sem,
            recv_sem=recv_sem,
            device_id={"reg": target},
            device_id_type=MESH,
        ).start()

    each_peer(peers, me, one)
    recv_buf[me] = send_buf[me]


def whole(peers, me, send_buf, recv_buf, send_sem, recv_sem):
    return pltpu.make_async_remote_copy(
        src_ref=send_buf.at[pl.ds(0, peers - 1)],
        dst_ref=recv_buf.at[pl.ds(0, peers - 1)],
        send_sem=send_sem,
        recv_sem=recv_sem,
        device_id={"reg": lax.rem(me + 1, peers)},
        device_id_type=MESH,
    )


def kernel(
    peers,
    comps,
    top_flow, mid_lp, low_lp, top_w, mid_w, top_ch, mid_ch,
    low_out, top_params, mid_params,
    flow_in, mid_in, low_in, tw, mw, tch, mch,
    stage, rows, edge_ids,
    pick_top, sum_top, pick_mid, sum_mid,
    w_turned, outers, lefts, rights, partials, mass_mid, flow_turned, ratios,
    moments, moments_in, params,
    s1m, r1m, s1l, r1l, s2t, r2t, s2m, r2m, s3, r3, s4, r4, s5, r5, s6, r6,
    in_sem, send_sem, recv_sem, mom_send, mom_recv, out_sem,
):
    me = lax.axis_index("reg")
    bat = lax.axis_index("bat")
    other = 1 - bat
    n_top = tw.shape[0]
    n_mid = mw.shape[0]
    n_low = low_in.shape[0]
    half = comps // 2
    pairs = flow_in.shape[1] // LANES
    wide = 2 * LANES

    loads = [
        pltpu.make_async_copy(src, dst, in_sem.at[slot])
        for slot, (src, dst) in enumerate(
            [(mid_lp, mid_in), (low_lp, low_in), (top_ch, tch), (mid_ch, mch),
             (top_flow, flow_in), (top_w, tw), (mid_w, mw)]
        )
    ]
    for load in loads:
        load.start()

    barrier = pltpu.get_barrier_semaphore()

    def greet(target):
        pl.semaphore_signal(barrier, inc=1, device_id={"reg": target}, device_id_type=MESH)

    each_peer(peers, me, greet)
    pl.semaphore_signal(barrier, inc=1, device_id={"bat": other}, device_id_type=MESH)

    def chunk_rows(source, count):
        def some(group, carry):
            for u in range(8):
                c = group * 8 + u
                stage[pl.ds(pl.multiple_of(c * 8, 8), count), :] = source[
                    :, pl.ds(pl.multiple_of(c * LANES, LANES), LANES)
                ]
            return carry

        lax.fori_loop(0, pairs // 8, some, 0)

    def values_to_send(source, count, send_buf):
        chunk_rows(source, count)
        slots = send_buf.shape[1]
        for q in range(slots):
            if q >= count:
                rows[pl.ds(q, LANES, stride=slots), :] = jnp.zeros((LANES, LANES), F32)
                continue
            turned = stage[pl.ds(q, LANES, stride=8), :].T
            parts = []
            for par in range(2):
                part = turned[par * comps:(par + 1) * comps]
                parts.append(jnp.exp(part - jnp.max(part, axis=0, keepdims=True)))
            rows[pl.ds(q, LANES, stride=slots), :] = jnp.concatenate(parts, axis=0)
        send_buf[...] = rows[0:LANES * slots].astype(send_buf.dtype).reshape(send_buf.shape)

    def edge_table(children, grouped, slots):
        ids = children[...]
        if grouped != slots:
            ids = (ids // grouped) * slots + ids % grouped
        ids = ids.astype(F32)
        for t in range(children.shape[1] // LANES):
            for side in range(2):
                block = jnp.broadcast_to(
                    ids[side:side + 1, t * LANES:(t + 1) * LANES], (LANES, LANES)
                )
                edge_ids[pl.ds(2 * t * LANES + side, LANES, stride=2), :] = block.T

    def pick_table(edges, pick):
        ids = edge_ids[0:edges]
        lane = lax.broadcasted_iota(jnp.int32, (edges, LANES), 1).astype(F32)
        for t in range(pick.shape[1] // LANES):
            pick[:, t * LANES:(t + 1) * LANES] = jnp.where(
                ids == lane + float(t * LANES), 1.0, 0.0
            ).astype(BF16)

    def sum_table(edges, table):
        count = table.shape[0]
        row = lax.broadcasted_iota(jnp.int32, (count, LANES), 0).astype(F32)
        for t in range(edges // LANES):
            turned = edge_ids[t * LANES:(t + 1) * LANES].T
            table[:, t * LANES:(t + 1) * LANES] = jnp.where(
                row == turned[0:1], 1.0, 0.0
            ).astype(BF16)

    def matrix(recv_buf):
        return recv_buf[...].reshape(recv_buf.shape[0] * recv_buf.shape[1], LANES)

    def product(a, b):
        return lax.dot_general(a, b, (((1,), (0,)), ((), ())), preferred_element_type=F32)

    def unpack(recv_buf):
        slots = recv_buf.shape[1]
        rows[0:LANES * slots] = recv_buf[...].astype(F32).reshape(LANES * slots, LANES)

    def wide_row(q, slots):
        return jnp.concatenate(
            [rows[pl.ds(par * comps * slots + q, comps, stride=slots), :] for par in range(2)], axis=1
        )

    def put_wide(q, slots, value):
        for par in range(2):
            rows[pl.ds(par * comps * slots + q, comps, stride=slots), :] = value[
                :, par * LANES:(par + 1) * LANES
            ]

    def pack(send_buf):
        slots = send_buf.shape[1]
        send_buf[...] = rows[0:LANES * slots].astype(send_buf.dtype).reshape(send_buf.shape)

    def build_outer(slot):
        right = rights[slot].astype(BF16).reshape(comps // 16, 16, wide)

        def some(group, carry):
            for u in range(4):
                i = group * 4 + u
                left = jnp.broadcast_to(lefts[slot, pl.ds(i, 1), :], (16, wide)).astype(BF16)
                outers[slot, pl.ds(pl.multiple_of(i * comps, comps), comps), :] = (
                    right * left[None]
                ).reshape(comps, wide)
            return carry

        lax.fori_loop(0, comps // 4, some, 0)

    def flows_of(slot, ratio, q, slots):
        right = rights[slot]

        def block(b, right_acc):
            start = pl.multiple_of(b * 8 * comps, 8 * comps)
            spread = product(w_turned[slot, pl.ds(start, 8 * comps), :], ratio)
            for u in range(8):
                piece = spread[u * comps:(u + 1) * comps]
                left = lefts[slot, pl.ds(b * 8 + u, 1), :]
                right_acc = right_acc + piece * left
                folded = jnp.sum((piece * right).reshape(comps // 8, 8, wide), axis=0)
                at = pl.ds(pl.multiple_of((b * 8 + u) * 8, 8), 8)
                for par in range(2):
                    partials[par, at, :] = folded[:, par * LANES:(par + 1) * LANES]
            return right_acc

        right_acc = lax.fori_loop(0, comps // 8, block, jnp.zeros((comps, wide), F32))
        left_acc = jnp.concatenate(
            [
                functools.reduce(
                    lambda a, b: a + b,
                    [partials[par, pl.ds(sub, comps, stride=8), :] for sub in range(8)],
                )
                for par in range(2)
            ],
            axis=1,
        )
        put_wide(q, slots, left_acc * lefts[slot])
        put_wide(q + 1, slots, right_acc * right)

    def moment_of(slot):
        moments[slot] = lax.dot_general(
            ratios[slot], outers[slot], (((1,), (1,)), ((), ())), preferred_element_type=F32
        )

    def moment_copy(slot):
        return pltpu.make_async_remote_copy(
            src_ref=moments.at[slot, pl.ds(pl.multiple_of(other * half, half), half), :],
            dst_ref=moments_in.at[slot],
            send_sem=mom_send.at[slot],
            recv_sem=mom_recv.at[slot],
            device_id={"bat": other},
            device_id_type=MESH,
        )

    def finish_params(slot, weight):
        moment_copy(slot).wait_recv()
        own = pl.ds(pl.multiple_of(bat * half, half), half)
        params[slot] = (moments[slot, own, :] + moments_in[slot]) * weight[own, :].astype(F32)

    def phase(index, send_buf, recv_buf):
        return (peers, me, send_buf, recv_buf, send_sem.at[index], recv_sem.at[index])

    phases = [
        phase(index, a, b)
        for index, (a, b) in enumerate(
            [(s1m, r1m), (s1l, r1l), (s2t, r2t), (s2m, r2m), (s3, r3), (s4, r4), (s5, r5), (s6, r6)]
        )
    ]

    loads[0].wait()
    values_to_send(mid_in, n_mid, s1m)
    loads[1].wait()
    values_to_send(low_in, n_low, s1l)
    pl.semaphore_wait(barrier, peers)
    exchange(*phases[0])
    exchange(*phases[1])

    loads[2].wait()
    edge_table(tch, n_mid, s1m.shape[1])
    pick_table(pick_top.shape[0], pick_top)

    whole(*phases[0]).wait_recv()
    s2t[...] = product(pick_top[...], matrix(r1m)).astype(BF16).reshape(s2t.shape)
    exchange(*phases[2])

    sum_table(pick_top.shape[0], sum_top)
    loads[3].wait()
    edge_table(mch, n_low, s1l.shape[1])
    pick_table(pick_mid.shape[0], pick_mid)
    whole(*phases[1]).wait_recv()
    s2m[...] = product(pick_mid[...], matrix(r1l)).astype(BF16).reshape(s2m.shape)
    exchange(*phases[3])

    loads[5].wait()
    for r in range(n_top):
        w_turned[r] = tw[r].T
    loads[4].wait()
    chunk_rows(flow_in, n_top)
    for r in range(n_top):
        turned = stage[pl.ds(r, LANES, stride=8), :].T
        flow_turned[r] = jnp.concatenate([turned[0:comps], turned[comps:2 * comps]], axis=1)

    whole(*phases[2]).wait_recv()
    unpack(r2t)
    for r in range(n_top):
        lefts[r] = wide_row(2 * r, 2 * n_top)
        rights[r] = wide_row(2 * r + 1, 2 * n_top)
    for r in range(n_top):
        build_outer(r)
        mass = product(tw[r], outers[r])
        ratio = (flow_turned[r] / mass).astype(BF16)
        ratios[r] = ratio
        flows_of(r, ratio, 2 * r, 2 * n_top)
    pack(s3)
    exchange(*phases[4])

    for r in range(n_top):
        moment_of(r)
        moment_copy(r).start()
    sum_table(pick_mid.shape[0], sum_mid)

    whole(*phases[4]).wait_recv()
    s4[...] = product(sum_top[...], matrix(r3)).reshape(s4.shape)
    exchange(*phases[5])

    loads[6].wait()
    whole(*phases[3]).wait_recv()
    unpack(r2m)
    for r in range(n_mid):
        lefts[n_top + r] = wide_row(2 * r, 2 * n_mid)
        rights[n_top + r] = wide_row(2 * r + 1, 2 * n_mid)
    for r in range(n_mid):
        w_turned[n_top + r] = mw[r].T
        build_outer(n_top + r)
        mass_mid[r] = product(mw[r], outers[n_top + r])

    whole(*phases[5]).wait_recv()
    unpack(r4)
    for r in range(n_mid):
        flow_turned[r] = wide_row(r, r4.shape[1])
    for r in range(n_mid):
        ratio = (flow_turned[r] / mass_mid[r]).astype(BF16)
        ratios[n_top + r] = ratio
        flows_of(n_top + r, ratio, 2 * r, 2 * n_mid)
    pack(s5)
    exchange(*phases[6])

    outs = []
    for r in range(n_top):
        finish_params(r, tw.at[r])
        outs.append(pltpu.make_async_copy(params.at[r], top_params.at[r], out_sem.at[r]))
        outs[-1].start()
    for r in range(n_mid):
        moment_of(n_top + r)
        moment_copy(n_top + r).start()

    whole(*phases[6]).wait_recv()
    s6[...] = product(sum_mid[...], matrix(r5)).reshape(s6.shape)
    exchange(*phases[7])

    for r in range(n_mid):
        slot = n_top + r
        finish_params(slot, mw.at[r])
        outs.append(pltpu.make_async_copy(params.at[slot], mid_params.at[r], out_sem.at[slot]))
        outs[-1].start()

    whole(*phases[7]).wait_recv()
    unpack(r6)
    for q in range(n_low):
        stage[pl.ds(q, LANES, stride=8), :] = rows[pl.ds(q, LANES, stride=n_low), :].T

    def some_out(group, carry):
        for u in range(8):
            c = group * 8 + u
            low_out[:, pl.ds(pl.multiple_of(c * LANES, LANES), LANES)] = stage[
                pl.ds(pl.multiple_of(c * 8, 8), n_low), :
            ]
        return carry

    lax.fori_loop(0, pairs // 8, some_out, 0)

    for one in phases:
        whole(*one).wait_send()
    for slot in range(n_top + n_mid):
        moment_copy(slot).wait_send()
    for out in outs:
        out.wait()


def shards(top_flow, mid_logprob, low_logprob, top_weight, mid_weight, top_children, mid_children):
    peers = lax.axis_size("reg")
    n_top, comps, square = top_weight.shape
    n_mid = mid_weight.shape[0]
    n_low = low_logprob.shape[0]
    n_all = n_top + n_mid
    half = comps // 2
    wide = 2 * LANES
    mid_slots = 4
    top_edges = 2 * n_top
    mid_edges = 2 * n_mid
    vmem = pltpu.VMEM

    def pair(slots, kind=BF16):
        return [vmem((peers, slots, LANES), kind)] * 2

    low, top_params, mid_params = pl.pallas_call(
        functools.partial(kernel, peers, comps),
        out_shape=(
            jax.ShapeDtypeStruct(low_logprob.shape, F32),
            jax.ShapeDtypeStruct((n_top, half, square), F32),
            jax.ShapeDtypeStruct((n_mid, half, square), F32),
        ),
        in_specs=[pl.BlockSpec(memory_space=pltpu.HBM)] * 7,
        out_specs=(
            pl.BlockSpec(memory_space=pltpu.VMEM),
            pl.BlockSpec(memory_space=pl.ANY),
            pl.BlockSpec(memory_space=pl.ANY),
        ),
        scratch_shapes=[
            vmem(top_flow.shape, F32),
            vmem(mid_logprob.shape, F32),
            vmem(low_logprob.shape, F32),
            vmem(top_weight.shape, BF16),
            vmem(mid_weight.shape, BF16),
            vmem(top_children.shape[::-1], jnp.int32),
            vmem(mid_children.shape[::-1], jnp.int32),
            vmem((8 * LANES, LANES), F32),
            vmem((LANES * mid_edges, LANES), F32),
            vmem((peers * mid_edges, LANES), F32),
            vmem((peers * top_edges, peers * mid_slots), BF16),
            vmem((peers * mid_slots, peers * top_edges), BF16),
            vmem((peers * mid_edges, peers * n_low), BF16),
            vmem((peers * n_low, peers * mid_edges), BF16),
            vmem((n_all, square, comps), BF16),
            vmem((n_all, square, wide), BF16),
            vmem((n_all, comps, wide), F32),
            vmem((n_all, comps, wide), F32),
            vmem((2, 8 * comps, LANES), F32),
            vmem((n_mid, comps, wide), F32),
            vmem((n_mid, comps, wide), F32),
            vmem((n_all, comps, wide), BF16),
            vmem((n_all, comps, square), F32),
            vmem((n_all, half, square), F32),
            vmem((n_all, half, square), F32),
            *pair(mid_slots), *pair(n_low), *pair(top_edges), *pair(mid_edges),
            *pair(top_edges), *pair(mid_slots, F32), *pair(mid_edges), *pair(n_low, F32),
            pltpu.SemaphoreType.DMA((7,)),
            pltpu.SemaphoreType.DMA((8,)),
            pltpu.SemaphoreType.DMA((8,)),
            pltpu.SemaphoreType.DMA((n_all,)),
            pltpu.SemaphoreType.DMA((n_all,)),
            pltpu.SemaphoreType.DMA((n_all,)),
        ],
        compiler_params=pltpu.CompilerParams(
            collective_id=0, has_side_effects=True, vmem_limit_bytes=60 * 1024 * 1024
        ),
    )(top_flow, mid_logprob, low_logprob, top_weight, mid_weight, top_children.T, mid_children.T)
    return low, top_params, mid_params


def solution(mesh):
    return jax.shard_map(
        shards,
        mesh=mesh,
        in_specs=(
            P("reg", "bat"),
            P("reg", "bat"),
            P("reg", "bat"),
            P("reg", None, None),
            P("reg", None, None),
            P(),
            P(),
        ),
        out_specs=(P("reg", "bat"), P("reg", "bat", None), P("reg", "bat", None)),
        check_vma=False,
    )
```

```python
import functools

import jax
import jax.numpy as jnp
from jax import lax
from jax.experimental import pallas as pl
from jax.experimental.pallas import tpu as pltpu
from jax.sharding import PartitionSpec as P

F32 = jnp.float32
BF16 = jnp.bfloat16
MESH = pl.DeviceIdType.MESH
LANES = 128


def each_peer(peers, me, visit):
    def one(step):
        ahead = me + step
        visit(jnp.where(ahead >= peers, ahead - peers, ahead))

    def some(group, carry):
        for u in range(1, 9):
            one(group * 8 + u)
        return carry

    groups = (peers - 1) // 8
    lax.fori_loop(0, groups, some, 0)
    for step in range(groups * 8 + 1, peers):
        one(step)


def exchange(peers, me, send_buf, recv_buf, send_sem, recv_sem):
    def one(target):
        pltpu.make_async_remote_copy(
            src_ref=send_buf.at[target],
            dst_ref=recv_buf.at[me],
            send_sem=send_sem,
            recv_sem=recv_sem,
            device_id={"reg": target},
            device_id_type=MESH,
        ).start()

    each_peer(peers, me, one)
    recv_buf[me] = send_buf[me]


def whole(peers, me, send_buf, recv_buf, send_sem, recv_sem):
    return pltpu.make_async_remote_copy(
        src_ref=send_buf.at[pl.ds(0, peers - 1)],
        dst_ref=recv_buf.at[pl.ds(0, peers - 1)],
        send_sem=send_sem,
        recv_sem=recv_sem,
        device_id={"reg": lax.rem(me + 1, peers)},
        device_id_type=MESH,
    )


def kernel(
    peers,
    comps,
    top_flow, mid_lp, low_lp, top_w, mid_w, top_ch, mid_ch,
    low_out, top_params, mid_params,
    flow_in, mid_in, low_in, tw, mw, tch, mch,
    stage, rows, edge_ids,
    pick_top, sum_top, pick_mid, sum_mid,
    w_turned, outers, lefts, rights, partials, mass_mid, flow_turned, ratios,
    moments, moments_in, params,
    s1m, r1m, s1l, r1l, s2t, r2t, s2m, r2m, s3, r3, s4, r4, s5, r5, s6, r6,
    in_sem, send_sem, recv_sem, mom_send, mom_recv, out_sem,
):
    me = lax.axis_index("reg")
    bat = lax.axis_index("bat")
    other = 1 - bat
    n_top = tw.shape[0]
    n_mid = mw.shape[0]
    n_low = low_in.shape[0]
    half = comps // 2
    pairs = flow_in.shape[1] // LANES
    wide = 2 * LANES

    loads = [
        pltpu.make_async_copy(src, dst, in_sem.at[slot])
        for slot, (src, dst) in enumerate(
            [(mid_lp, mid_in), (low_lp, low_in), (top_ch, tch), (mid_ch, mch),
             (top_flow, flow_in), (top_w, tw), (mid_w, mw)]
        )
    ]
    for load in loads:
        load.start()

    barrier = pltpu.get_barrier_semaphore()

    def greet(target):
        pl.semaphore_signal(barrier, inc=1, device_id={"reg": target}, device_id_type=MESH)

    each_peer(peers, me, greet)
    pl.semaphore_signal(barrier, inc=1, device_id={"bat": other}, device_id_type=MESH)

    def chunk_rows(source, count):
        def some(group, carry):
            for u in range(8):
                c = group * 8 + u
                stage[pl.ds(pl.multiple_of(c * 8, 8), count), :] = source[
                    :, pl.ds(pl.multiple_of(c * LANES, LANES), LANES)
                ]
            return carry

        lax.fori_loop(0, pairs // 8, some, 0)

    def values_to_send(source, count, send_buf):
        chunk_rows(source, count)
        slots = send_buf.shape[1]
        for q in range(slots):
            if q >= count:
                rows[pl.ds(q, LANES, stride=slots), :] = jnp.zeros((LANES, LANES), F32)
                continue
            turned = stage[pl.ds(q, LANES, stride=8), :].T
            parts = []
            for par in range(2):
                part = turned[par * comps:(par + 1) * comps]
                parts.append(jnp.exp(part - jnp.max(part, axis=0, keepdims=True)))
            rows[pl.ds(q, LANES, stride=slots), :] = jnp.concatenate(parts, axis=0)
        send_buf[...] = rows[0:LANES * slots].astype(send_buf.dtype).reshape(send_buf.shape)

    def edge_table(children, grouped, slots):
        ids = children[...]
        if grouped != slots:
            ids = (ids // grouped) * slots + ids % grouped
        ids = ids.astype(F32)
        for t in range(children.shape[1] // LANES):
            for side in range(2):
                block = jnp.broadcast_to(
                    ids[side:side + 1, t * LANES:(t + 1) * LANES], (LANES, LANES)
                )
                edge_ids[pl.ds(2 * t * LANES + side, LANES, stride=2), :] = block.T

    def pick_table(edges, pick):
        ids = edge_ids[0:edges]
        lane = lax.broadcasted_iota(jnp.int32, (edges, LANES), 1).astype(F32)
        for t in range(pick.shape[1] // LANES):
            pick[:, t * LANES:(t + 1) * LANES] = jnp.where(
                ids == lane + float(t * LANES), 1.0, 0.0
            ).astype(BF16)

    def sum_table(edges, table):
        count = table.shape[0]
        row = lax.broadcasted_iota(jnp.int32, (count, LANES), 0).astype(F32)
        for t in range(edges // LANES):
            turned = edge_ids[t * LANES:(t + 1) * LANES].T
            table[:, t * LANES:(t + 1) * LANES] = jnp.where(
                row == turned[0:1], 1.0, 0.0
            ).astype(BF16)

    def matrix(recv_buf):
        return recv_buf[...].reshape(recv_buf.shape[0] * recv_buf.shape[1], LANES)

    def product(a, b):
        return lax.dot_general(a, b, (((1,), (0,)), ((), ())), preferred_element_type=F32)

    def unpack(recv_buf):
        slots = recv_buf.shape[1]
        rows[0:LANES * slots] = recv_buf[...].astype(F32).reshape(LANES * slots, LANES)

    def wide_row(q, slots):
        return jnp.concatenate(
            [rows[pl.ds(par * comps * slots + q, comps, stride=slots), :] for par in range(2)], axis=1
        )

    def put_wide(q, slots, value):
        for par in range(2):
            rows[pl.ds(par * comps * slots + q, comps, stride=slots), :] = value[
                :, par * LANES:(par + 1) * LANES
            ]

    def pack(send_buf):
        slots = send_buf.shape[1]
        send_buf[...] = rows[0:LANES * slots].astype(send_buf.dtype).reshape(send_buf.shape)

    def build_outer(slot):
        right = rights[slot].astype(BF16).reshape(comps // 16, 16, wide)

        def some(group, carry):
            for u in range(4):
                i = group * 4 + u
                left = jnp.broadcast_to(lefts[slot, pl.ds(i, 1), :], (16, wide)).astype(BF16)
                outers[slot, pl.ds(pl.multiple_of(i * comps, comps), comps), :] = (
                    right * left[None]
                ).reshape(comps, wide)
            return carry

        lax.fori_loop(0, comps // 4, some, 0)

    def flows_of(slot, ratio, q, slots):
        right = rights[slot]

        def block(b, right_acc):
            start = pl.multiple_of(b * 8 * comps, 8 * comps)
            spread = product(w_turned[slot, pl.ds(start, 8 * comps), :], ratio)
            for u in range(8):
                piece = spread[u * comps:(u + 1) * comps]
                left = lefts[slot, pl.ds(b * 8 + u, 1), :]
                right_acc = right_acc + piece * left
                folded = jnp.sum((piece * right).reshape(comps // 8, 8, wide), axis=0)
                at = pl.ds(pl.multiple_of((b * 8 + u) * 8, 8), 8)
                for par in range(2):
                    partials[par, at, :] = folded[:, par * LANES:(par + 1) * LANES]
            return right_acc

        right_acc = lax.fori_loop(0, comps // 8, block, jnp.zeros((comps, wide), F32))
        left_acc = jnp.concatenate(
            [
                functools.reduce(
                    lambda a, b: a + b,
                    [partials[par, pl.ds(sub, comps, stride=8), :] for sub in range(8)],
                )
                for par in range(2)
            ],
            axis=1,
        )
        put_wide(q, slots, left_acc * lefts[slot])
        put_wide(q + 1, slots, right_acc * right)

    def moment_of(slot):
        moments[slot] = lax.dot_general(
            ratios[slot], outers[slot], (((1,), (1,)), ((), ())), preferred_element_type=F32
        )

    def moment_copy(slot):
        return pltpu.make_async_remote_copy(
            src_ref=moments.at[slot, pl.ds(pl.multiple_of(other * half, half), half), :],
            dst_ref=moments_in.at[slot],
            send_sem=mom_send.at[slot],
            recv_sem=mom_recv.at[slot],
            device_id={"bat": other},
            device_id_type=MESH,
        )

    def finish_params(slot, weight):
        moment_copy(slot).wait_recv()
        own = pl.ds(pl.multiple_of(bat * half, half), half)
        params[slot] = (moments[slot, own, :] + moments_in[slot]) * weight[own, :].astype(F32)

    def phase(index, send_buf, recv_buf):
        return (peers, me, send_buf, recv_buf, send_sem.at[index], recv_sem.at[index])

    phases = [
        phase(index, a, b)
        for index, (a, b) in enumerate(
            [(s1m, r1m), (s1l, r1l), (s2t, r2t), (s2m, r2m), (s3, r3), (s4, r4), (s5, r5), (s6, r6)]
        )
    ]

    loads[0].wait()
    values_to_send(mid_in, n_mid, s1m)
    pl.semaphore_wait(barrier, peers)
    exchange(*phases[0])
    loads[1].wait()
    values_to_send(low_in, n_low, s1l)
    exchange(*phases[1])

    loads[2].wait()
    edge_table(tch, n_mid, s1m.shape[1])
    pick_table(pick_top.shape[0], pick_top)

    whole(*phases[0]).wait_recv()
    s2t[...] = product(pick_top[...], matrix(r1m)).astype(BF16).reshape(s2t.shape)
    exchange(*phases[2])

    sum_table(pick_top.shape[0], sum_top)
    loads[5].wait()
    for r in range(n_top):
        w_turned[r] = tw[r].T
    loads[4].wait()
    chunk_rows(flow_in, n_top)
    for r in range(n_top):
        turned = stage[pl.ds(r, LANES, stride=8), :].T
        flow_turned[r] = jnp.concatenate([turned[0:comps], turned[comps:2 * comps]], axis=1)

    whole(*phases[2]).wait_recv()
    unpack(r2t)
    for r in range(n_top):
        lefts[r] = wide_row(2 * r, 2 * n_top)
        rights[r] = wide_row(2 * r + 1, 2 * n_top)
    for r in range(n_top):
        build_outer(r)
        mass = product(tw[r], outers[r])
        ratio = (flow_turned[r] / mass).astype(BF16)
        ratios[r] = ratio
        flows_of(r, ratio, 2 * r, 2 * n_top)
    pack(s3)
    exchange(*phases[4])

    loads[3].wait()
    edge_table(mch, n_low, s1l.shape[1])
    pick_table(pick_mid.shape[0], pick_mid)
    whole(*phases[1]).wait_recv()
    s2m[...] = product(pick_mid[...], matrix(r1l)).astype(BF16).reshape(s2m.shape)
    exchange(*phases[3])
    for r in range(n_top):
        moment_of(r)
        moment_copy(r).start()
    sum_table(pick_mid.shape[0], sum_mid)

    whole(*phases[4]).wait_recv()
    s4[...] = product(sum_top[...], matrix(r3)).reshape(s4.shape)
    exchange(*phases[5])

    loads[6].wait()
    whole(*phases[3]).wait_recv()
    unpack(r2m)
    for r in range(n_mid):
        lefts[n_top + r] = wide_row(2 * r, 2 * n_mid)
        rights[n_top + r] = wide_row(2 * r + 1, 2 * n_mid)
    for r in range(n_mid):
        w_turned[n_top + r] = mw[r].T
        build_outer(n_top + r)
        mass_mid[r] = product(mw[r], outers[n_top + r])

    whole(*phases[5]).wait_recv()
    unpack(r4)
    for r in range(n_mid):
        flow_turned[r] = wide_row(r, r4.shape[1])
    for r in range(n_mid):
        ratio = (flow_turned[r] / mass_mid[r]).astype(BF16)
        ratios[n_top + r] = ratio
        flows_of(n_top + r, ratio, 2 * r, 2 * n_mid)
    pack(s5)
    exchange(*phases[6])

    outs = []
    for r in range(n_top):
        finish_params(r, tw.at[r])
        outs.append(pltpu.make_async_copy(params.at[r], top_params.at[r], out_sem.at[r]))
        outs[-1].start()
    for r in range(n_mid):
        moment_of(n_top + r)
        moment_copy(n_top + r).start()

    whole(*phases[6]).wait_recv()
    s6[...] = product(sum_mid[...], matrix(r5)).reshape(s6.shape)
    exchange(*phases[7])

    for r in range(n_mid):
        slot = n_top + r
        finish_params(slot, mw.at[r])
        outs.append(pltpu.make_async_copy(params.at[slot], mid_params.at[r], out_sem.at[slot]))
        outs[-1].start()

    whole(*phases[7]).wait_recv()
    unpack(r6)
    for q in range(n_low):
        stage[pl.ds(q, LANES, stride=8), :] = rows[pl.ds(q, LANES, stride=n_low), :].T

    def some_out(group, carry):
        for u in range(8):
            c = group * 8 + u
            low_out[:, pl.ds(pl.multiple_of(c * LANES, LANES), LANES)] = stage[
                pl.ds(pl.multiple_of(c * 8, 8), n_low), :
            ]
        return carry

    lax.fori_loop(0, pairs // 8, some_out, 0)

    for one in phases:
        whole(*one).wait_send()
    for slot in range(n_top + n_mid):
        moment_copy(slot).wait_send()
    for out in outs:
        out.wait()


def shards(top_flow, mid_logprob, low_logprob, top_weight, mid_weight, top_children, mid_children):
    peers = lax.axis_size("reg")
    n_top, comps, square = top_weight.shape
    n_mid = mid_weight.shape[0]
    n_low = low_logprob.shape[0]
    n_all = n_top + n_mid
    half = comps // 2
    wide = 2 * LANES
    mid_slots = 4
    top_edges = 2 * n_top
    mid_edges = 2 * n_mid
    vmem = pltpu.VMEM

    def pair(slots, kind=BF16):
        return [vmem((peers, slots, LANES), kind)] * 2

    low, top_params, mid_params = pl.pallas_call(
        functools.partial(kernel, peers, comps),
        out_shape=(
            jax.ShapeDtypeStruct(low_logprob.shape, F32),
            jax.ShapeDtypeStruct((n_top, half, square), F32),
            jax.ShapeDtypeStruct((n_mid, half, square), F32),
        ),
        in_specs=[pl.BlockSpec(memory_space=pltpu.HBM)] * 7,
        out_specs=(
            pl.BlockSpec(memory_space=pltpu.VMEM),
            pl.BlockSpec(memory_space=pl.ANY),
            pl.BlockSpec(memory_space=pl.ANY),
        ),
        scratch_shapes=[
            vmem(top_flow.shape, F32),
            vmem(mid_logprob.shape, F32),
            vmem(low_logprob.shape, F32),
            vmem(top_weight.shape, BF16),
            vmem(mid_weight.shape, BF16),
            vmem(top_children.shape[::-1], jnp.int32),
            vmem(mid_children.shape[::-1], jnp.int32),
            vmem((8 * LANES, LANES), F32),
            vmem((LANES * mid_edges, LANES), F32),
            vmem((peers * mid_edges, LANES), F32),
            vmem((peers * top_edges, peers * mid_slots), BF16),
            vmem((peers * mid_slots, peers * top_edges), BF16),
            vmem((peers * mid_edges, peers * n_low), BF16),
            vmem((peers * n_low, peers * mid_edges), BF16),
            vmem((n_all, square, comps), BF16),
            vmem((n_all, square, wide), BF16),
            vmem((n_all, comps, wide), F32),
            vmem((n_all, comps, wide), F32),
            vmem((2, 8 * comps, LANES), F32),
            vmem((n_mid, comps, wide), F32),
            vmem((n_mid, comps, wide), F32),
            vmem((n_all, comps, wide), BF16),
            vmem((n_all, comps, square), F32),
            vmem((n_all, half, square), F32),
            vmem((n_all, half, square), F32),
            *pair(mid_slots), *pair(n_low), *pair(top_edges), *pair(mid_edges),
            *pair(top_edges), *pair(mid_slots, F32), *pair(mid_edges), *pair(n_low, F32),
            pltpu.SemaphoreType.DMA((7,)),
            pltpu.SemaphoreType.DMA((8,)),
            pltpu.SemaphoreType.DMA((8,)),
            pltpu.SemaphoreType.DMA((n_all,)),
            pltpu.SemaphoreType.DMA((n_all,)),
            pltpu.SemaphoreType.DMA((n_all,)),
        ],
        compiler_params=pltpu.CompilerParams(
            collective_id=0, has_side_effects=True, vmem_limit_bytes=60 * 1024 * 1024
        ),
    )(top_flow, mid_logprob, low_logprob, top_weight, mid_weight, top_children.T, mid_children.T)
    return low, top_params, mid_params


def solution(mesh):
    return jax.shard_map(
        shards,
        mesh=mesh,
        in_specs=(
            P("reg", "bat"),
            P("reg", "bat"),
            P("reg", "bat"),
            P("reg", None, None),
            P("reg", None, None),
            P(),
            P(),
        ),
        out_specs=(P("reg", "bat"), P("reg", "bat", None), P("reg", "bat", None)),
        check_vma=False,
    )
```
